32 devices in a mesh: tensor: 8 (over z, x), context: 4 (over y, core).
Axes of the slice: x: 2, y: 2, z: 4, core: 2. Of those that a mesh axis runs over, the one named last changes fastest.
Arguments:
- xs: bfloat16 [2048, 8192], P('context', 'tensor'), may hold values from -6 to 6
- bcs: bfloat16 [2048, 2048], P('context'), may hold values from -6 to 6
- zs: bfloat16 [2048, 8192], P('context', 'tensor'), may hold values from -13.8 to 13.8
- dt_raw: float32 [2048, 128], P('context', 'tensor'), may hold values from -3 to 12, as said below
- conv_x: float32 [4, 8192], P(None, 'tensor'), may hold values from -3 to 3
- conv_bc: float32 [4, 2048], replicated, may hold values from -3 to 3
- dt_bias: float32 [128], P('tensor'), may hold values from -6 to -5
- a_log: float32 [128], P('tensor'), may hold values from -3.51 to 2.31
- skip_d: float32 [128], P('tensor'), may hold values from 1 to 3
- norm_gain: float32 [8192], P('tensor'), may hold values from 0.1 to 1.9
- w_out: bfloat16 [8192, 8192], P('tensor'), may hold values from -0.0625 to 0.0625
- resid: bfloat16 [2048, 8192], P(('context', 'tensor')), may hold values from -6 to 6
- attn_gain: float32 [8192], replicated, may hold values from 0.1 to 1.9
- w_q: bfloat16 [8192, 4096], P(None, 'tensor')
- w_kv: bfloat16 [8192, 2048], P('tensor')
Outputs:
- mamba_hidden: bfloat16 [2048, 8192], P(('context', 'tensor'))
- attn_heads: bfloat16 [2048, 4096], P('context', 'tensor')
The draws below stay inside these ranges and needn't reach their ends.
Inputs may be any that keep to these rules, and one draw needn't show every extreme that they name: `dt_raw`: step size logits of order one with a few large positive rows.
All inputs are finite; a program needn't handle non-finite values.
Results may differ from the reference program's by a relative error of at most 0.006.
Values may be sent and summed in bfloat16 or wider, within the bound.
No kernel may reach another device: no remote copies, remote signals or barrier semaphores. Data moves between devices by JAX's collectives and lax.ppermute only.
A program may use at most 192 MiB of HBM per device.

```python
import jax
import jax.numpy as jnp
from jax import lax

D = 8192
HEADS = 128
P_SIZE = 64
NST = 256
G = 4
KW = 4
QH = 32
KVH = 8
HD = 128
TOK_DEV = 512
WINDOW_TOKENS = 2048
HP = 8192


def draw_zs(key, part):
    columns = jnp.arange(HEADS * P_SIZE)
    fraction = columns.astype(jnp.float32) / (HEADS * P_SIZE)
    base = jnp.clip(jax.random.normal(key, (WINDOW_TOKENS, HEADS * P_SIZE), jnp.float32), -6.0, 6.0)
    column_scale = 0.6 * 3.0 ** fraction
    return (base * column_scale[None, :]).astype(jnp.bfloat16)


def draw_dt_raw(key, part):
    random_offsets = 0.5 * jnp.clip(jax.random.normal(jax.random.fold_in(key, 1), (WINDOW_TOKENS, HEADS), jnp.float32), -6.0, 6.0)
    segment_rows = jax.random.randint(jax.random.fold_in(key, 2), (3,), 0, WINDOW_TOKENS)
    token_places = jnp.arange(WINDOW_TOKENS)
    segments = jnp.any(token_places[:, None] == segment_rows[None, :], axis=1).astype(jnp.float32)
    return random_offsets + 9.0 * segments[:, None]


def draw_a_log(key, part):
    picks = jax.random.randint(jax.random.fold_in(key, 1), (HEADS,), 0, 10)
    fast = picks < 5
    fast_log = jax.random.uniform(jax.random.fold_in(key, 2), (HEADS,), jnp.float32, 1.3863, 2.3026)
    slow_log = jax.random.uniform(jax.random.fold_in(key, 3), (HEADS,), jnp.float32, -3.5066, -2.5257)
    return jnp.where(fast, fast_log, slow_log)


def attention_weights(key):
    kv_part = jnp.clip(jax.random.normal(jax.random.fold_in(key, 11), (D, 2 * KVH * HD), jnp.float32), -6.0, 6.0) * D ** (-0.5)
    random_offsets = jnp.clip(jax.random.normal(jax.random.fold_in(key, 12), (D, QH * HD), jnp.float32), -6.0, 6.0) * D ** (-0.5)
    query_part = random_offsets
    return (query_part, kv_part)


def draw_w_q(key, part):
    return attention_weights(key)[0].astype(jnp.bfloat16)


def draw_w_kv(key, part):
    return attention_weights(key)[1].astype(jnp.bfloat16)


def block_scale(key, extent, split, smallest, largest):
    def one(position, parts):
        steps = jax.random.uniform(jax.random.fold_in(jax.random.fold_in(key, 6), position), (parts,), jnp.float32, smallest / len(split), largest / len(split))
        return jnp.repeat(jnp.exp(steps), extent[position] // parts).reshape((-1,) + (1,) * (len(extent) - position - 1))

    level = one(*split[0])
    for cut in split[1:]:
        level = level * one(*cut)
    return level


def bell_draw(own_key, dims, scale, most, shards=(), held_as=jnp.bfloat16):
    loudness = block_scale(own_key, dims, shards, -0.22, 0.18) if shards else 1.0
    values = jax.random.normal(own_key, dims, jnp.float32) * scale * loudness
    return jnp.minimum(jnp.maximum(values, -most), most).astype(held_as)


def setup_inputs(seed: int = 0) -> dict:
    key_list = jax.random.split(jax.random.key(seed), 16)
    xs = bell_draw(key_list[0], (WINDOW_TOKENS, HP), 1.0, 6.0, ((0, 4), (1, 8)))
    bcs = bell_draw(key_list[1], (WINDOW_TOKENS, 2 * G * NST), 1.0, 6.0, ((0, 4),))
    zs = draw_zs(jax.random.fold_in(key_list[15], 71), 0)
    dt_raw = draw_dt_raw(jax.random.fold_in(key_list[15], 71), 0)
    conv_x = bell_draw(key_list[4], (KW, HP), KW ** -0.5, 3.0, ((1, 8),), jnp.float32)
    conv_bc = bell_draw(key_list[5], (KW, 2 * G * NST), KW ** -0.5, 3.0, (), jnp.float32)
    dt_bias = jnp.clip(-6.0 + 1.0 * jax.random.uniform(key_list[6], (HEADS,), jnp.float32) ** block_scale(key_list[6], (HEADS,), ((0, 8),), -0.2, 0.2), -6.0, -5.0)
    a_log = draw_a_log(jax.random.fold_in(key_list[15], 71), 0)
    skip_d = jnp.clip(1.0 + 2.0 * jax.random.uniform(key_list[8], (HEADS,), jnp.float32) ** block_scale(key_list[8], (HEADS,), ((0, 8),), -0.2, 0.2), 1.0, 3.0)
    norm_gain = jnp.clip(1.0 + 0.18 * jax.random.normal(key_list[9], (HP,), jnp.float32), 0.1, 1.9)
    w_out = bell_draw(key_list[10], (HP, D), HP ** -0.5, 0.0625, ((0, 8),))
    resid = bell_draw(key_list[11], (WINDOW_TOKENS, D), 1.0, 6.0, ((0, 32),))
    attn_gain = jnp.clip(1.0 + 0.18 * jax.random.normal(key_list[12], (D,), jnp.float32), 0.1, 1.9)
    w_q = draw_w_q(jax.random.fold_in(key_list[15], 71), 0)
    w_kv = draw_w_kv(jax.random.fold_in(key_list[15], 71), 0)
    return {"xs": xs, "bcs": bcs, "zs": zs, "dt_raw": dt_raw, "conv_x": conv_x, "conv_bc": conv_bc, "dt_bias": dt_bias, "a_log": a_log, "skip_d": skip_d, "norm_gain": norm_gain, "w_out": w_out, "resid": resid, "attn_gain": attn_gain, "w_q": w_q, "w_kv": w_kv}


highest = lax.Precision.HIGHEST
epsilon = 1e-05

def causal_taps(values, taps):
    total_rows = values.shape[0]
    rim_rows = jnp.zeros((taps.shape[0] - 1, values.shape[1]), jnp.float32)
    padded = jnp.concatenate([rim_rows, values.astype(jnp.float32)], axis=0)
    total = jnp.zeros((total_rows, values.shape[1]), jnp.float32)
    for tap_index in range(taps.shape[0]):
        total = total + taps[tap_index] * padded[tap_index:tap_index + total_rows]
    return total

def rms_scaled(hidden, gain):
    values = hidden.astype(jnp.float32)
    mean_of_squares = lax.optimization_barrier(jnp.mean(values * values, axis=1, keepdims=True))
    return (values * lax.rsqrt(mean_of_squares + epsilon) * gain).astype(jnp.bfloat16)

def group_scan(operands):
    heads_x, dt_step, rates, b_mat, c_mat, skips = operands
    blocks = WINDOW_TOKENS // TOK_DEV
    per_group = heads_x.shape[1]
    block_x = heads_x.reshape(blocks, TOK_DEV, per_group, P_SIZE)
    block_dt = dt_step.reshape(blocks, TOK_DEV, per_group)
    block_b = b_mat.reshape(blocks, TOK_DEV, NST)
    block_c = c_mat.reshape(blocks, TOK_DEV, NST)
    lower_mask = (jnp.arange(TOK_DEV)[:, None] >= jnp.arange(TOK_DEV)[None, :])[:, :, None]

    def one_block(state, pieces):
        x_part, dt_part, b_part, c_part = pieces
        cumul = jnp.cumsum(-dt_part * rates[None, :], axis=0)
        spread = cumul[:, None, :] - cumul[None, :, :]
        decay = jnp.where(lower_mask, jnp.exp(jnp.where(lower_mask, spread, 0.0)), 0.0)
        inner_cb = jnp.dot(c_part, b_part.T, precision=highest)
        mixing = inner_cb[:, :, None] * decay * dt_part[None, :, :]
        y_inner = jnp.einsum('tsh,shp->thp', mixing, x_part, precision=highest)
        y_state = jnp.einsum('tn,hpn->thp', c_part, state, precision=highest) * jnp.exp(cumul)[:, :, None]
        y_total = y_inner + y_state + skips[None, :, None] * x_part
        end_weight = jnp.exp(cumul[-1][None, :] - cumul) * dt_part
        local_state = jnp.einsum('shp,sn->hpn', end_weight[:, :, None] * x_part, b_part, precision=highest)
        new_state = jnp.exp(cumul[-1])[:, None, None] * state + local_state
        return (new_state, y_total)
    start_state = jnp.zeros((per_group, P_SIZE, NST), jnp.float32)
    final_state, outputs = lax.scan(one_block, start_state, (block_x, block_dt, block_b, block_c))
    return outputs.reshape(WINDOW_TOKENS, per_group, P_SIZE)

def reference(xs, bcs, zs, dt_raw, conv_x, conv_bc, dt_bias, a_log, skip_d, norm_gain, w_out, resid, attn_gain, w_q, w_kv):
    per_group = HEADS // G
    x_conv = jax.nn.silu(causal_taps(xs, conv_x))
    bc_conv = jax.nn.silu(causal_taps(bcs, conv_bc))
    b_mat = bc_conv[:, :G * NST].reshape(WINDOW_TOKENS, G, NST)
    c_mat = bc_conv[:, G * NST:].reshape(WINDOW_TOKENS, G, NST)
    dt_step = jax.nn.softplus(dt_raw + dt_bias)
    rates = jnp.exp(a_log)
    grouped_x = x_conv.reshape(WINDOW_TOKENS, G, per_group, P_SIZE).transpose(1, 0, 2, 3)
    grouped_dt = dt_step.reshape(WINDOW_TOKENS, G, per_group).transpose(1, 0, 2)
    ssm_out = lax.map(group_scan, (grouped_x, grouped_dt, rates.reshape(G, per_group), b_mat.transpose(1, 0, 2), c_mat.transpose(1, 0, 2), skip_d.reshape(G, per_group)))
    ssm_out = ssm_out.transpose(1, 0, 2, 3).reshape(WINDOW_TOKENS, HEADS * P_SIZE)
    gated = ssm_out * jax.nn.silu(zs.astype(jnp.float32))
    grouped = gated.reshape(WINDOW_TOKENS, HEADS // G, G, P_SIZE)
    mean_of_squares = lax.optimization_barrier(jnp.mean(grouped * grouped, axis=(1, 3), keepdims=True))
    ynorm = ((grouped * lax.rsqrt(mean_of_squares + epsilon)).reshape(WINDOW_TOKENS, HEADS * P_SIZE) * norm_gain).astype(jnp.bfloat16)
    mixed = jnp.dot(ynorm, w_out, preferred_element_type=jnp.float32)
    mamba_hidden = (resid.astype(jnp.float32) + mixed).astype(jnp.bfloat16)
    normed = rms_scaled(mamba_hidden, attn_gain)
    queries = jnp.dot(normed, w_q, preferred_element_type=jnp.float32).astype(jnp.bfloat16).reshape(WINDOW_TOKENS, QH, HD)
    kvs = jnp.dot(normed, w_kv, preferred_element_type=jnp.float32).astype(jnp.bfloat16).reshape(WINDOW_TOKENS, KVH, 2, HD)
    token_places = jnp.arange(WINDOW_TOKENS, dtype=jnp.int32)
    allowed = token_places[None, :] <= token_places[:, None]
    score_scale = float(HD) ** (-0.5)
    ratio = QH // KVH

    def one_head(head_index):
        query_head = lax.dynamic_index_in_dim(queries, head_index, 1, keepdims=False)
        pair = lax.dynamic_index_in_dim(kvs, head_index // ratio, 1, keepdims=False)
        scores = jnp.dot(query_head, pair[:, 0].T, preferred_element_type=jnp.float32) * score_scale
        scores = jnp.where(allowed, scores, -jnp.inf)
        row_max = lax.optimization_barrier(jnp.max(scores, axis=1, keepdims=True))
        weights = jnp.exp(scores - row_max)
        totals = lax.optimization_barrier(jnp.sum(weights, axis=1, keepdims=True))
        probs = weights.astype(jnp.bfloat16)
        return jnp.dot(probs, pair[:, 1], preferred_element_type=jnp.float32) / totals
    heads_out = lax.map(one_head, jnp.arange(QH, dtype=jnp.int32))
    attn_heads = heads_out.transpose(1, 0, 2).reshape(WINDOW_TOKENS, QH * HD).astype(jnp.bfloat16)
    return (mamba_hidden, attn_heads)
```

```python
import jax
import jax.numpy as jnp
from jax import lax
from jax.experimental import pallas as pl
from jax.experimental.pallas import tpu as pltpu
from jax.sharding import PartitionSpec as P

HEADS = 128
P_SIZE = 64
NST = 256
G = 4
QH = 32
KVH = 8
HD = 128
ZDIM = 4
CHUNKS = 4

highest = lax.Precision.HIGHEST
epsilon = 1e-05
f32 = jnp.float32
bf16 = jnp.bfloat16


def dyn(arr, start, size, axis):
    return lax.dynamic_slice_in_dim(arr, start, size, axis)


def pick(arr, i, axis=0):
    return lax.dynamic_index_in_dim(arr, i, axis, keepdims=False)


def xor_swap(value, axis, mask):
    size = lax.axis_size(axis)
    return lax.ppermute(value, axis, [(i, i ^ mask) for i in range(size)])


def from_behind(shard, axis, by):
    size = lax.axis_size(axis)
    pairs = [(i, i + by) for i in range(size - by)]
    return lax.ppermute(shard, axis, pairs)


def gathered_weights(w_q, w_kv, tpos, core, xdim):
    tdim = ZDIM * xdim
    x = tpos % xdim
    feats = w_q.shape[0] // xdim
    half = feats // 2
    got_q = []
    for s in range(1, xdim):
        mine = dyn(w_q, (x ^ s) * feats + core * half, half, 0)
        got_q.append(lax.ppermute(mine, "tensor", [(i, i ^ s) for i in range(tdim)]))
    rows = w_kv.shape[0]
    h = tpos // ZDIM
    u = tpos % ZDIM
    qheads_dev = w_q.shape[1] // HD
    rows_half = dyn(w_kv, core * (rows // 2), rows // 2, 0)
    got = []
    for s in range(ZDIM):
        zt = u ^ s
        cols = []
        for s2 in range(xdim):
            owner = zt * xdim + (h ^ s2)
            head = owner * qheads_dev // (QH // KVH)
            cols.append(dyn(rows_half, head * 2 * HD, 2 * HD, 1))
        send = jnp.concatenate(cols, axis=1)
        perm = [(i, ((i % ZDIM) ^ s) * xdim + i // ZDIM) for i in range(tdim)]
        got.append(lax.ppermute(send, "tensor", perm))
    got = jnp.stack(got)
    wkv = jnp.stack([got, xor_swap(got, "context", 1)])
    if xdim == 1:
        return None, wkv
    got_q = jnp.stack(got_q)
    return jnp.stack([got_q, xor_swap(got_q, "context", 1)], axis=1), wkv


def gathered_resid(resid, tpos, xdim):
    x = tpos % xdim
    feats = resid.shape[1] // xdim
    parts = [dyn(resid, x * feats, feats, 1)]
    for s in range(1, xdim):
        parts.append(xor_swap(dyn(resid, (x ^ s) * feats, feats, 1), "tensor", s))
    parts = jnp.stack(parts)
    return jnp.concatenate([pick(parts, x ^ v) for v in range(xdim)], axis=0)


def entry_of(total, state, context_pos):
    pairs = lax.axis_size("context") // 2
    core = context_pos % 2
    wide = lambda t: jnp.repeat(jnp.exp(t[:1]), P_SIZE, axis=1)
    sib_total, sib_state = xor_swap((total, state.astype(bf16)), "context", 1)
    sib_state = sib_state.astype(f32)
    first = core == 0
    t0, s0 = jnp.where(first, total, sib_total), jnp.where(first, state, sib_state)
    t1, s1 = jnp.where(first, sib_total, total), jnp.where(first, sib_state, state)
    chip_total = t0 + t1
    chip_state = (wide(t1) * s0 + s1).astype(bf16)
    entry = jnp.zeros_like(state)
    weight = jnp.zeros_like(total)
    for k in range(1, pairs):
        far = from_behind(chip_state, "context", 2 * k).astype(f32)
        entry = entry + (far if k == 1 else wide(weight) * far)
        if k + 1 < pairs:
            weight = weight + from_behind(chip_total, "context", 2 * k)
    return jnp.where(first, entry, wide(t0) * entry + s0).astype(bf16)


def tensor_sum(value):
    step = 1
    while step < lax.axis_size("tensor"):
        value = value + xor_swap(value, "tensor", step)
        step *= 2
    return value


ROWS = 128


def mm(a, b, dims=((1,), (0,)), precision=highest):
    return lax.dot_general(a, b, (dims, ((), ())), precision=precision, preferred_element_type=f32)


def one_hot_rows(rows, cols, f):
    r = lax.broadcasted_iota(jnp.int32, (rows, cols), 0)
    c = lax.broadcasted_iota(jnp.int32, (rows, cols), 1)
    return jnp.where(f(r, c), 1.0, 0.0).astype(f32)


def silu(v):
    return v / (1.0 + jnp.exp(-v))


def ssm_local_kernel(
    grp, xs, bs, cs, rim, tx, tb, tc, dtr, dtb, al, sk, y, c_out, eg, st_out, tot_out, px, pb, pc, st, off
):
    i = pl.program_id(0)
    chan = xs.shape[1]
    heads = dtr.shape[1]

    @pl.when(i == 0)
    def _():
        px[0:8, :] = rim[:, :chan].astype(f32)
        pb[0:8, :] = rim[:, chan : chan + NST].astype(f32)
        pc[0:8, :] = rim[:, chan + NST :].astype(f32)
        st[...] = jnp.zeros_like(st)
        off[...] = jnp.zeros_like(off)

    def conv(pad, new, taps):
        pad[8 : 8 + ROWS, :] = new[...].astype(f32)
        total = taps[0:1, :] * pad[5 : 5 + ROWS, :]
        for k in range(1, 4):
            total = total + taps[k : k + 1, :] * pad[5 + k : 5 + k + ROWS, :]
        pad[0:8, :] = pad[ROWS : ROWS + 8, :]
        return silu(total)

    x = conv(px, xs, tx)
    b = conv(pb, bs, tb)
    c = conv(pc, cs, tc)
    c_out[...] = c
    v = dtr[...] + dtb[...]
    dt = jnp.maximum(v, 0.0) + jnp.log1p(jnp.exp(-jnp.abs(v)))
    a = -dt * jnp.exp(al[...])
    tri = one_hot_rows(ROWS, ROWS, lambda r, q: r >= q)
    mask = tri > 0.5
    cum = mm(tri, a)
    cum_t = cum.T
    spread_heads = one_hot_rows(heads, chan, lambda r, q: q // P_SIZE == r)
    xd = x * mm(dt, spread_heads)
    last = cum[ROWS - 1 : ROWS, :]
    weighted = xd * mm(jnp.exp(last - cum), spread_heads)
    cb = mm(c, b, ((1,), (1,)))
    base = mm(c, st[...]) * mm(jnp.exp(cum), spread_heads) + mm(
        jnp.broadcast_to(sk[...], (8, heads)), spread_heads
    )[0:1, :] * x
    low = lax.broadcasted_iota(jnp.int32, (ROWS, 2 * P_SIZE), 1) < P_SIZE
    for p in range(heads // 2):
        lanes = slice(2 * p * P_SIZE, 2 * (p + 1) * P_SIZE)
        mixes = []
        for h in (2 * p, 2 * p + 1):
            gap = cum[:, h : h + 1] - cum_t[h : h + 1, :]
            mixes.append(cb * jnp.exp(jnp.where(mask, gap, -1e30)))
        xp = xd[:, lanes]
        both = jnp.concatenate([jnp.where(low, xp, 0.0), jnp.where(low, 0.0, xp)], axis=0)
        y[:, lanes] = base[:, lanes] + mm(jnp.concatenate(mixes, axis=1), both)
    step = mm(jnp.broadcast_to(jnp.exp(last), (8, heads)), spread_heads)[0:1, :]
    st[...] = st[...] * step + mm(b, weighted, ((0,), (0,)))
    eg[...] = jnp.exp(off[0:1, :] + cum)
    off[...] = off[...] + last
    st_out[...] = st[...]
    tot_out[...] = off[...]


def ssm_local(group_idx, xs, bcs, rim, conv_x, conv_bc, dt_raw, dt_bias, a_log, skip_d):
    rows, chan = xs.shape
    heads = dt_raw.shape[1]
    whole = lambda shape: pl.BlockSpec(shape, lambda i, g: (0, 0))
    by_row = lambda cols: pl.BlockSpec((ROWS, cols), lambda i, g: (i, 0))
    return pl.pallas_call(
        ssm_local_kernel,
        grid_spec=pltpu.PrefetchScalarGridSpec(
            num_scalar_prefetch=1,
            grid=(rows // ROWS,),
            in_specs=[
                by_row(chan),
                pl.BlockSpec((ROWS, NST), lambda i, g: (i, g[0])),
                pl.BlockSpec((ROWS, NST), lambda i, g: (i, G + g[0])),
                whole(rim.shape),
                whole(conv_x.shape),
                pl.BlockSpec((conv_bc.shape[0], NST), lambda i, g: (0, g[0])),
                pl.BlockSpec((conv_bc.shape[0], NST), lambda i, g: (0, G + g[0])),
                by_row(heads),
                whole((1, heads)),
                whole((1, heads)),
                whole((1, heads)),
            ],
            out_specs=[by_row(chan), by_row(NST), by_row(heads), whole((NST, chan)), whole((8, heads))],
            scratch_shapes=[
                pltpu.VMEM((ROWS + 8, chan), f32),
                pltpu.VMEM((ROWS + 8, NST), f32),
                pltpu.VMEM((ROWS + 8, NST), f32),
                pltpu.VMEM((NST, chan), f32),
                pltpu.VMEM((8, heads), f32),
            ],
        ),
        out_shape=[
            jax.ShapeDtypeStruct((rows, chan), f32),
            jax.ShapeDtypeStruct((rows, NST), f32),
            jax.ShapeDtypeStruct((rows, heads), f32),
            jax.ShapeDtypeStruct((NST, chan), f32),
            jax.ShapeDtypeStruct((8, heads), f32),
        ],
    )(
        group_idx.reshape(1), xs, bcs, bcs, rim, conv_x, conv_bc, conv_bc, dt_raw,
        dt_bias[None, :], a_log[None, :], skip_d[None, :],
    )


def class_rows(chan):
    return one_hot_rows(8, chan, lambda r, q: (q // P_SIZE) % G == r)


def ssm_gate_kernel(y, c, eg, entry, zs, gated, table):
    chan = y.shape[1]
    heads = eg.shape[1]
    spread_heads = one_hot_rows(heads, chan, lambda r, q: q // P_SIZE == r)
    out = y[...] + mm(c[...], entry[...].astype(f32)) * mm(eg[...], spread_heads)
    out = out * silu(zs[...].astype(f32))
    gated[...] = out
    table[...] = mm(class_rows(chan), out * out, ((1,), (1,)))


def ssm_gate(y, c, eg, entry, zs):
    rows, chan = y.shape
    by_row = lambda cols: pl.BlockSpec((ROWS, cols), lambda i: (i, 0))
    return pl.pallas_call(
        ssm_gate_kernel,
        grid=(rows // ROWS,),
        in_specs=[by_row(chan), by_row(NST), by_row(eg.shape[1]), pl.BlockSpec(entry.shape, lambda i: (0, 0)), by_row(chan)],
        out_specs=[by_row(chan), pl.BlockSpec((8, ROWS), lambda i: (0, i))],
        out_shape=[jax.ShapeDtypeStruct((rows, chan), f32), jax.ShapeDtypeStruct((8, rows), f32)],
    )(y, c, eg, entry, zs)


def ynorm_kernel(gated, sums, gain, out):
    chan = gated.shape[1]
    scale = lax.rsqrt(sums[...] / (HEADS * P_SIZE // G) + epsilon)
    wide = mm(scale, class_rows(chan), ((0,), (0,)))
    out[...] = (gated[...] * wide * gain[...]).astype(bf16).reshape(out.shape)


def ynorm_of(gated, sums, gain):
    rows, chan = gated.shape
    part = rows // ZDIM
    return pl.pallas_call(
        ynorm_kernel,
        grid=(ZDIM,),
        in_specs=[
            pl.BlockSpec((part, chan), lambda v: (v, 0)),
            pl.BlockSpec((8, part), lambda v: (0, v)),
            pl.BlockSpec((1, chan), lambda v: (0, 0)),
        ],
        out_specs=pl.BlockSpec((CHUNKS, 1, part // CHUNKS, chan), lambda v: (0, v, 0, 0)),
        out_shape=jax.ShapeDtypeStruct((CHUNKS, ZDIM, part // CHUNKS, chan), bf16),
    )(gated, sums, gain[None, :])


def out_proj_kernel(idx, y, w, *outs):
    for i, out in enumerate(outs):
        out[...] = jnp.dot(y[i], w[...], preferred_element_type=f32).astype(out.dtype)


def out_proj(y, w_out, block, feats, dtype):
    tile = 512
    per = feats // tile
    chunks, rows, chan = y.shape
    return pl.pallas_call(
        out_proj_kernel,
        grid_spec=pltpu.PrefetchScalarGridSpec(
            num_scalar_prefetch=1,
            grid=(per,),
            in_specs=[
                pl.BlockSpec((chunks, rows, chan), lambda j, b: (0, 0, 0)),
                pl.BlockSpec((chan, tile), lambda j, b: (0, b[0] * per + j)),
            ],
            out_specs=[pl.BlockSpec((rows, tile), lambda j, b: (0, j))] * chunks,
        ),
        out_shape=[jax.ShapeDtypeStruct((rows, feats), dtype)] * chunks,
    )(block.reshape(1), y, w_out)


def make_proj(xdim, qcols):
    cols = qcols + 2 * HD

    def kernel(idx, own, far, gain, wq, *rest):
        rest = list(rest)
        wqx = rest.pop(0) if xdim > 1 else None
        wkv = rest.pop(0)
        keep, sums = rest.pop(0), rest.pop(0)
        msg = rest.pop(0) if xdim > 1 else None
        acc, sq = rest
        j = pl.program_id(0)

        @pl.when(j == 0)
        def _():
            acc[...] = jnp.zeros_like(acc)
            sq[...] = jnp.zeros_like(sq)

        flat = jnp.concatenate([own[0], own[1], far[0], far[1]], axis=0).astype(f32)
        sq[...] = sq[...] + jnp.sum(flat * flat, axis=1, keepdims=True)
        scaled = (flat * gain[...]).astype(bf16)
        kv = jnp.dot(scaled, wkv[0, 0], preferred_element_type=f32)
        for s in range(xdim):
            w = wq[...] if s == 0 else wqx[s - 1, 0]
            acc[:, s * cols : s * cols + qcols] += jnp.dot(scaled, w, preferred_element_type=f32)
            acc[:, s * cols + qcols : (s + 1) * cols] += kv[:, s * 2 * HD : (s + 1) * 2 * HD]

        @pl.when(j == pl.num_programs(0) - 1)
        def _():
            keep[...] = acc[:, :cols].reshape(keep.shape)
            total = sq[...]
            sums[...] = total.reshape(sums.shape)
            hi = total.astype(bf16).astype(f32)
            mid = (total - hi).astype(bf16).astype(f32)
            low = total - hi - mid
            lane = lax.broadcasted_iota(jnp.int32, (total.shape[0], HD), 1)
            packed = jnp.where(lane == 0, hi, jnp.where(lane == 1, mid, jnp.where(lane == 2, low, 0.0)))
            for s in range(1, xdim):
                msg[s - 1, :, :, :cols] = acc[:, s * cols : (s + 1) * cols].astype(bf16).reshape(msg.shape[1], msg.shape[2], cols)
                msg[s - 1, :, :, cols:] = packed.astype(bf16).reshape(msg.shape[1], msg.shape[2], HD)

    return kernel


def project(own, far, gain, w_q, wq_far, wkv, x, z, core):
    _, sub, feats = own.shape
    qcols = w_q.shape[1]
    xdim = w_q.shape[0] // feats
    cols = qcols + 2 * HD
    kb = wkv.shape[2]
    steps = feats // kb
    half = steps // 2
    piece = pl.BlockSpec((2, sub, kb), lambda j, s: (0, 0, j))
    in_specs = [piece, piece, pl.BlockSpec((1, kb), lambda j, s: (0, s[0] * steps + j)),
                pl.BlockSpec((kb, qcols), lambda j, s: (s[0] * steps + j, 0))]
    args = [own, far, gain[None, :], w_q]
    out_specs = [pl.BlockSpec((ZDIM, sub, cols), lambda j, s: (0, 0, 0)),
                 pl.BlockSpec((ZDIM, sub, 1), lambda j, s: (0, 0, 0))]
    out_shape = [jax.ShapeDtypeStruct((ZDIM, sub, cols), f32), jax.ShapeDtypeStruct((ZDIM, sub, 1), f32)]
    if xdim > 1:
        in_specs.append(pl.BlockSpec((xdim - 1, 1, kb, qcols), lambda j, s: (0, (j // half) ^ s[2], j % half, 0)))
        args.append(wq_far)
        out_specs.append(pl.BlockSpec((xdim - 1, ZDIM, sub, cols + HD), lambda j, s: (0, 0, 0, 0)))
        out_shape.append(jax.ShapeDtypeStruct((xdim - 1, ZDIM, sub, cols + HD), bf16))
    in_specs.append(pl.BlockSpec((1, 1, kb, xdim * 2 * HD), lambda j, s: ((j % 2) ^ s[2], (j // 2) ^ s[1], 0, 0)))
    args.append(wkv)
    out = pl.pallas_call(
        make_proj(xdim, qcols),
        grid_spec=pltpu.PrefetchScalarGridSpec(
            num_scalar_prefetch=1, grid=(steps,), in_specs=in_specs, out_specs=out_specs,
            scratch_shapes=[pltpu.VMEM((ZDIM * sub, xdim * cols), f32), pltpu.VMEM((ZDIM * sub, 1), f32)],
        ),
        out_shape=out_shape,
    )(jnp.stack([x, z, core]), *args)
    return out[0], out[1], (out[2] if xdim > 1 else None)


def finish(parts, z, qcols, model, slab_rows):
    cols = qcols + 2 * HD
    sub = parts[0][0].shape[1]
    far = parts[0][2].shape[0]

    def kernel(idx, *refs):
        q, kv = refs[-2:]
        for i in range(CHUNKS):
            keep, sums, got = refs[3 * i : 3 * i + 3]
            own = keep[0]
            total = sums[0]
            for s in range(far):
                m = got[s, 0].astype(f32)
                own = own + m[:, :cols]
                total = total + (m[:, cols : cols + 1] + m[:, cols + 1 : cols + 2] + m[:, cols + 2 : cols + 3])
            own = (own * lax.rsqrt(total / model + epsilon)).astype(bf16)
            q[i * sub : (i + 1) * sub, :] = own[:, :qcols]
            kv[i * sub : (i + 1) * sub, :] = own[:, qcols:]

    rel = lambda v, s: 2 * ((v % 2) ^ (s[0] % 2)) + ((v // 2) ^ (s[0] // 2))
    in_specs = []
    args = []
    for part in parts:
        in_specs += [pl.BlockSpec((1, sub, cols), lambda v, s: (rel(v, s), 0, 0)),
                     pl.BlockSpec((1, sub, 1), lambda v, s: (rel(v, s), 0, 0)),
                     pl.BlockSpec((far, 1, sub, cols + HD), lambda v, s: (0, rel(v, s), 0, 0))]
        args += list(part)
    rows = CHUNKS * sub
    return pl.pallas_call(
        kernel,
        grid_spec=pltpu.PrefetchScalarGridSpec(
            num_scalar_prefetch=1, grid=(ZDIM,), in_specs=in_specs,
            out_specs=[pl.BlockSpec((rows, qcols), lambda v, s: (v, 0)), pl.BlockSpec((rows, 2 * HD), lambda v, s: (v, 0))],
        ),
        out_shape=[jax.ShapeDtypeStruct((slab_rows, qcols), bf16), jax.ShapeDtypeStruct((slab_rows, 2 * HD), bf16)],
    )(z.reshape(1), *args)


def attend(q, kv, slabs, me, heads):
    rows = q.shape[0]
    count = kv.shape[0]
    scale = float(HD) ** (-0.5)

    def kernel(idx, q_ref, kv_ref, out, top, tot, acc):
        j = pl.program_id(0)

        @pl.when(j == 0)
        def _():
            row = lax.broadcasted_iota(jnp.int32, (rows, rows), 0)
            col = lax.broadcasted_iota(jnp.int32, (rows, rows), 1)
            mask = col <= row
            for h in range(heads):
                s = mm(q_ref[:, h * HD : (h + 1) * HD], kv_ref[0, :, :HD], ((1,), (1,)), None) * scale
                s = jnp.where(mask, s, -1e30)
                m = jnp.max(s, axis=1, keepdims=True)
                p = jnp.exp(s - m)
                top[h] = m
                tot[h] = jnp.sum(p, axis=1, keepdims=True)
                acc[h] = jnp.dot(p.astype(bf16), kv_ref[0, :, HD:], preferred_element_type=f32)

        @pl.when((j > 0) & (idx[j] >= 0) & (idx[j] < idx[0]))
        def _():
            for h in range(heads):
                s = mm(q_ref[:, h * HD : (h + 1) * HD], kv_ref[0, :, :HD], ((1,), (1,)), None) * scale
                old = top[h]
                m = jnp.maximum(old, jnp.max(s, axis=1, keepdims=True))
                p = jnp.exp(s - m)
                fade = jnp.exp(old - m)
                top[h] = m
                tot[h] = tot[h] * fade + jnp.sum(p, axis=1, keepdims=True)
                acc[h] = acc[h] * fade + jnp.dot(p.astype(bf16), kv_ref[0, :, HD:], preferred_element_type=f32)

        @pl.when(j == count - 1)
        def _():
            for h in range(heads):
                out[:, h * HD : (h + 1) * HD] = (acc[h] / tot[h]).astype(bf16)

    return pl.pallas_call(
        kernel,
        grid_spec=pltpu.PrefetchScalarGridSpec(
            num_scalar_prefetch=1,
            grid=(count,),
            in_specs=[
                pl.BlockSpec(q.shape, lambda j, s: (0, 0)),
                pl.BlockSpec((1, rows, 2 * HD), lambda j, s: (j, 0, 0)),
            ],
            out_specs=pl.BlockSpec(q.shape, lambda j, s: (0, 0)),
            scratch_shapes=[
                pltpu.VMEM((heads, rows, 1), f32),
                pltpu.VMEM((heads, rows, 1), f32),
                pltpu.VMEM((heads, rows, HD), f32),
            ],
        ),
        out_shape=jax.ShapeDtypeStruct(q.shape, bf16),
    )(slabs, q, kv)


def shards(
    xs, bcs, zs, dt_raw, conv_x, conv_bc, dt_bias, a_log, skip_d, norm_gain, w_out, resid,
    attn_gain, w_q, w_kv,
):
    tpos = lax.axis_index("tensor")
    context_pos = lax.axis_index("context")
    core = context_pos % 2
    tdim = lax.axis_size("tensor")
    xdim = tdim // ZDIM
    x = tpos % xdim
    z = tpos // xdim
    zb0 = z % 2
    zb1 = z // 2
    slab_rows, chan_dev = xs.shape
    heads_dev = dt_raw.shape[1]
    group_idx = tpos * heads_dev // (HEADS // G)
    last = slab_rows - 8
    tail = jnp.concatenate(
        [xs[last:], dyn(bcs[last:], group_idx * NST, NST, 1), dyn(bcs[last:], G * NST + group_idx * NST, NST, 1)],
        axis=1,
    )
    rim = from_behind(tail, "context", 1)
    wq_far, wkv = gathered_weights(w_q, w_kv, tpos, core, xdim)
    resid_z = gathered_resid(resid, tpos, xdim)
    y_local, c_mat, decays, state, total = ssm_local(
        group_idx, xs, bcs, rim, conv_x, conv_bc, dt_raw, dt_bias, a_log, skip_d
    )
    entry = entry_of(total, state, context_pos)
    gated, table = ssm_gate(y_local, c_mat, decays, entry, zs)
    ynorm = ynorm_of(gated, tensor_sum(table), norm_gain)

    model = w_out.shape[1]
    feats = model // xdim
    qcols = w_q.shape[1]
    sub = slab_rows // (ZDIM * CHUNKS)
    yv = ynorm.reshape(CHUNKS, ZDIM * sub, chan_dev)
    rv = resid_z.reshape(CHUNKS, sub, feats)
    sends = [out_proj(yv, w_out, x ^ s, feats, bf16) for s in range(1, xdim)]
    keeps = out_proj(yv, w_out, x, feats, f32)

    def stage_x(i):
        total = keeps[i]
        for s in range(1, xdim):
            total = total + xor_swap(sends[s - 1][i], "tensor", s).astype(f32)
        return total.reshape(2, 2, sub, feats)

    def stage_z1(total):
        send = pick(total, 1 - zb0, 1).astype(bf16)
        return pick(total, zb0, 1) + xor_swap(send, "tensor", xdim).astype(f32)

    def stage_z2(total, i):
        send = pick(total, 1 - zb1, 0).astype(bf16)
        total = pick(total, zb1, 0) + xor_swap(send, "tensor", 2 * xdim).astype(f32)
        return (rv[i].astype(f32) + total).astype(bf16)

    hidden_parts = []
    parts = []
    for i in range(CHUNKS):
        hidden = stage_z2(stage_z1(stage_x(i)), i)
        hidden_parts.append(hidden)
        pair = jnp.stack([hidden, xor_swap(hidden, "tensor", 2 * xdim)])
        far = xor_swap(pair, "tensor", xdim)
        keep, sums, msg = project(pair, far, attn_gain, w_q, wq_far, wkv, x, z, core)
        got = jnp.stack([xor_swap(msg[s - 1], "tensor", s) for s in range(1, xdim)])
        parts.append((keep, sums, got))
    hidden_all = jnp.stack(hidden_parts).reshape(xdim, slab_rows // tdim, feats)
    outs = [pick(hidden_all, x)]
    for s in range(1, xdim):
        outs.append(xor_swap(pick(hidden_all, x ^ s), "tensor", s))
    outs = jnp.stack(outs)
    mamba_hidden = jnp.concatenate([pick(outs, x ^ v) for v in range(xdim)], axis=1)

    query_local, kv_own = finish(parts, z, qcols, model, slab_rows)
    pairs = lax.axis_size("context") // 2
    kv_list = [kv_own] + [from_behind(kv_own, "context", 2 * k) for k in range(1, pairs)]
    kv_stack = jnp.stack(kv_list)
    kv_all = jnp.concatenate([kv_stack, xor_swap(kv_stack, "context", 1)], axis=0)
    own_places = 2 * (context_pos // 2 - jnp.arange(pairs)) + core
    places = jnp.concatenate([own_places, own_places + 1 - 2 * core])
    attn_heads = attend(query_local, kv_all, places, context_pos, qcols // HD)
    return (mamba_hidden, attn_heads)


def solution(mesh):
    in_specs = (
        P("context", "tensor"),
        P("context", None),
        P("context", "tensor"),
        P("context", "tensor"),
        P(None, "tensor"),
        P(),
        P("tensor"),
        P("tensor"),
        P("tensor"),
        P("tensor"),
        P("tensor", None),
        P(("context", "tensor"), None),
        P(),
        P(None, "tensor"),
        P("tensor", None),
    )
    out_specs = (P(("context", "tensor"), None), P("context", "tensor"))
    return jax.shard_map(shards, mesh=mesh, in_specs=in_specs, out_specs=out_specs, check_vma=False)
```
